32 devices in a mesh: ctx: 4 (over y, core), tp: 4 (over z), dp: 2 (over x).
Axes of the slice: x: 2, y: 2, z: 4, core: 2. Of those that a mesh axis runs over, the one named last changes fastest.
Arguments:
- tokens: bfloat16 [3072, 3584], P(('dp', 'ctx'), 'tp'), may hold values from -6 to 6
- expert_ids: int32 [3072, 8], P(('dp', 'ctx')), may hold values from 0 to 255, all different within a row; in each aligned block of 384 rows (0 to 383, 384 to 767, ...) at most 24 rows name the same one
- gate_codes: int32 [3072, 8], P(('dp', 'ctx')), may hold values from 1 to 32767
- up_weight: bfloat16 [4, 3584, 1024], P('ctx', 'tp', 'dp'), may hold values from -0.09375 to 0.09375
- down_weight: bfloat16 [4, 1024, 3584], P('ctx', 'dp', 'tp'), may hold values from -0.1875 to 0.1875
- cotangent: bfloat16 [3072, 3584], P(('dp', 'ctx'), 'tp'), may hold values from -6 to 6
Outputs:
- mixed: bfloat16 [3072, 3584], P(('dp', 'ctx'), 'tp')
- grad_tokens: bfloat16 [3072, 3584], P(('dp', 'ctx'), 'tp')
- grad_up: bfloat16 [4, 3584, 1024], P('ctx', 'tp', 'dp')
- grad_down: bfloat16 [4, 1024, 3584], P('ctx', 'dp', 'tp')
The draws below stay inside these ranges and needn't reach their ends.
Inputs may be any that keep to these rules, and one draw needn't show every extreme that they name: `expert_ids`: each row names 8 different experts; among the 384 rows of one device no expert is named more than 24 times.
All inputs are finite; a program needn't handle non-finite values.
Results may differ from the reference program's by a relative error of at most 0.0066.
Values may be sent and summed in bfloat16 or wider, within the bound.
A program may use at most 64 MiB of HBM per device.

```python
import math
import jax
import jax.numpy as jnp
import numpy as np
from jax import lax

D = 3584
HW = 1024
ALL_EXPERTS = 256
TOPK = 8
TOK_DEV = 384
EXPERTS = 4
CAP = 24
TOKENS = 3072
N_DP = 2


def place_ends(values, own_key, smallest, top_value):
    place = [jax.random.randint(jax.random.fold_in(own_key, axis), (), 0, length) for axis, length in enumerate(values.shape)]
    main_axis = values.shape.index(max(values.shape))
    beside = place[:main_axis] + [(place[main_axis] + 1) % values.shape[main_axis]] + place[main_axis + 1:]
    return values.at[tuple(place)].set(smallest).at[tuple(beside)].set(top_value)


def shard_levels(stream_key, shape, pieces, least, top_value):
    def one(dim, blocks):
        steps = jax.random.uniform(jax.random.fold_in(jax.random.fold_in(stream_key, 6), dim), (blocks,), jnp.float32, least / len(pieces), top_value / len(pieces))
        return jnp.repeat(jnp.exp(steps), shape[dim] // blocks).reshape((-1,) + (1,) * (len(shape) - dim - 1))

    loudness = one(*pieces[0])
    for cut in pieces[1:]:
        loudness = loudness * one(*cut)
    return loudness


def assign_block(own_key, own, number, rows, count, top, reach, slope):
    sequence = jax.random.permutation(own_key, count)
    packed, ordinary = portions_of(count, rows * top, reach, slope, True), portions_of(count, rows * top, reach, slope, False)
    places = jnp.arange(count)

    def named(tallies, turn):
        used = int((tallies > 0).sum())
        fixed = max(1, used // 4)
        passed = fixed + (places - fixed + turn * (used - fixed)) % max(1, count - fixed)
        return jnp.zeros((count,), jnp.int32).at[sequence[jnp.where(places < fixed, places, passed)]].set(jnp.asarray(tallies, jnp.int32))

    tallies = jnp.where(number % 4 == 0, named(packed, number // 4), named(ordinary, number - number // 4 - 1))
    mixed = jax.random.permutation(jax.random.fold_in(own, 3), count)
    source_of, sink = mixed[0:count // 2 * 2:2], mixed[1:count // 2 * 2:2]
    slack = jnp.minimum(tallies[source_of] - 1, reach - tallies[sink]) // 2
    slack = jnp.where((source_of == sequence[0]) | (sink == sequence[0]) | (tallies[sink] == 0), 0, jnp.maximum(slack, 0))
    passed = jax.random.randint(jax.random.fold_in(own, 4), (count // 2,), 0, 1 << 20) % (slack + 1)
    tallies = tallies.at[source_of].add(-passed).at[sink].add(passed)
    members = jnp.searchsorted(jnp.cumsum(tallies), jnp.arange(rows * top), side="right").astype(jnp.int32)
    grid = members.reshape(top, rows).T
    grid = grid[jax.random.permutation(jax.random.fold_in(own, 1), rows)]
    turn = jax.random.randint(jax.random.fold_in(own, 2), (rows, 1), 0, top)
    return jnp.take_along_axis(grid, (jnp.arange(top)[None, :] + turn) % top, axis=1)


def portions_of(amount, total, reach, lean, full):
    weights = [(1 << 20) // math.isqrt(grade ** lean) + 1 for grade in range(1, amount + 1)]
    largest = reach if full else min(reach, max(-(-total // amount), total * weights[0] // sum(weights)))
    least = 1 if total - largest >= amount - 1 else 0
    given, rest = [largest] + [least] * (amount - 1), total - largest - least * (amount - 1)
    while rest > 0:
        free = [i for i in range(1, amount) if given[i] < largest] or [i for i in range(1, amount) if given[i] < reach]
        pool, budget = sum([weights[i] for i in free]), rest
        for i in free:
            addition = min(reach - given[i], max(1, budget * weights[i] // pool), rest)
            given[i] = given[i] + addition
            rest = rest - addition
    return np.array(given)


def normal_values(rng, shape, scale, bound, split=(), held_as=jnp.bfloat16):
    result = jax.random.normal(rng, shape, jnp.float32) * scale
    if len(split) > 0:
        result = shard_levels(rng, shape, split, -0.22, 0.18) * result
    return jnp.clip(result, min=-bound, max=bound).astype(held_as)


def setup_inputs(seed: int = 0) -> dict:
    keys = jax.random.split(jax.random.key(seed), 7)
    tokens = normal_values(keys[0], (TOKENS, D), 1.0, 6.0, ((0, 8), (1, 4)))
    expert_ids_keys = jax.random.split(jax.random.fold_in(keys[1], 1), TOKENS // TOK_DEV)
    expert_ids_turns = jax.random.permutation(jax.random.fold_in(keys[1], 3), TOKENS // TOK_DEV)
    expert_ids = jax.vmap(lambda own, number: assign_block(jax.random.fold_in(keys[1], 2), own, number, TOK_DEV, ALL_EXPERTS, TOPK, CAP, 2))(expert_ids_keys, expert_ids_turns).reshape((TOKENS, TOPK))
    gate_codes = place_ends(jax.random.randint(keys[2], (TOKENS, TOPK), 1, 32768), jax.random.fold_in(keys[2], 1), 1, 32767).astype(jnp.int32)
    up_weight = normal_values(keys[3], (EXPERTS, D, HW), D ** -0.5, 0.09375, ((0, 4), (1, 4), (2, 2)))
    down_weight = normal_values(keys[4], (EXPERTS, HW, D), HW ** -0.5, 0.1875, ((0, 4), (1, 2), (2, 4)))
    cotangent = normal_values(keys[5], (TOKENS, D), 1.0, 6.0, ((0, 8), (1, 4)))
    return {"tokens": tokens, "expert_ids": expert_ids, "gate_codes": gate_codes, "up_weight": up_weight, "down_weight": down_weight, "cotangent": cotangent}


def place_slots(expert_ids, gate_codes, experts, capacity):
    rows_count, picks = expert_ids.shape
    flat_ids = expert_ids.reshape(-1)
    one_hot = (flat_ids[:, None] == jnp.arange(experts, dtype=jnp.int32)[None, :]).astype(jnp.int32)
    before = jnp.cumsum(one_hot, axis=0) - one_hot
    slot_rank = lax.optimization_barrier(jnp.sum(before * one_hot, axis=1))
    inside = flat_ids < experts
    target = jnp.where(inside, flat_ids * capacity + slot_rank, experts * capacity).astype(jnp.int32)
    source = (jnp.arange(rows_count * picks, dtype=jnp.int32) // picks).astype(jnp.int32)
    slot_token = jnp.full((experts * capacity,), rows_count, jnp.int32).at[target].set(source, mode='drop')
    weights = gate_codes.reshape(-1).astype(jnp.float32) / 32768.0
    gate_slot = jnp.zeros((experts * capacity,), jnp.float32).at[target].set(weights, mode='drop')
    return (slot_token, gate_slot)

def silu_grad(values):
    sigma = jax.nn.sigmoid(values)
    return sigma * (1.0 + values * (1.0 - sigma))

def reference(tokens, expert_ids, gate_codes, up_weight, down_weight, cotangent):
    blocks = TOKENS // TOK_DEV
    ids_blocks = expert_ids.reshape(blocks, TOK_DEV, TOPK)
    code_blocks = gate_codes.reshape(blocks, TOK_DEV, TOPK)
    local_token, gate_slot = jax.vmap(lambda first, second: place_slots(first, second, EXPERTS, CAP))(ids_blocks, code_blocks)
    offsets = jnp.arange(blocks, dtype=jnp.int32)[:, None] * TOK_DEV
    global_token = jnp.where(local_token < TOK_DEV, local_token + offsets, TOKENS).astype(jnp.int32)
    global_token = global_token.reshape(blocks, EXPERTS, CAP).transpose(1, 0, 2).reshape(EXPERTS, blocks * CAP)
    gate_table = gate_slot.reshape(blocks, EXPERTS, CAP).transpose(1, 0, 2).reshape(EXPERTS, blocks * CAP)
    padded_x = jnp.concatenate([tokens, jnp.zeros((1, D), tokens.dtype)], axis=0)
    padded_c = jnp.concatenate([cotangent, jnp.zeros((1, D), cotangent.dtype)], axis=0)

    def expert_work(operands):
        index, gate, w_up, w_down = operands
        rows = padded_x[index]
        hidden = jnp.dot(rows, w_up, preferred_element_type=jnp.float32)
        active = jax.nn.silu(hidden).astype(jnp.bfloat16)
        produced = jnp.dot(active, w_down, preferred_element_type=jnp.float32).astype(jnp.bfloat16)
        grad_out = (gate[:, None] * padded_c[index].astype(jnp.float32)).astype(jnp.bfloat16)
        grad_act = jnp.dot(grad_out, w_down.T, preferred_element_type=jnp.float32)
        grad_hid = (grad_act * silu_grad(hidden)).astype(jnp.bfloat16)
        grad_in = jnp.dot(grad_hid, w_up.T, preferred_element_type=jnp.float32).astype(jnp.bfloat16)
        rows_g = rows.reshape(N_DP, -1, D).astype(jnp.float32)
        hid_g = grad_hid.reshape(N_DP, -1, HW).astype(jnp.float32)
        act_g = active.reshape(N_DP, -1, HW).astype(jnp.float32)
        out_g = grad_out.reshape(N_DP, -1, D).astype(jnp.float32)
        part_up = jnp.einsum('grj,gri->gji', rows_g, hid_g).astype(jnp.bfloat16)
        part_down = jnp.einsum('gri,grj->gij', act_g, out_g).astype(jnp.bfloat16)
        part_up, part_down = lax.optimization_barrier((part_up, part_down))
        grad_up = lax.optimization_barrier(jnp.sum(part_up.astype(jnp.float32), axis=0)).astype(jnp.bfloat16)
        grad_down = lax.optimization_barrier(jnp.sum(part_down.astype(jnp.float32), axis=0)).astype(jnp.bfloat16)
        return (produced, grad_in, grad_up, grad_down)
    produced, grad_in, grad_up, grad_down = lax.map(expert_work, (global_token, gate_table, up_weight, down_weight))
    flat_index = global_token.reshape(-1)
    flat_gate = gate_table.reshape(-1)
    mixed = jnp.zeros((TOKENS + 1, D), jnp.float32).at[flat_index].add(flat_gate[:, None] * produced.reshape(-1, D).astype(jnp.float32))
    grad_tokens = jnp.zeros((TOKENS + 1, D), jnp.float32).at[flat_index].add(grad_in.reshape(-1, D).astype(jnp.float32))
    return (mixed[:TOKENS].astype(jnp.bfloat16), grad_tokens[:TOKENS].astype(jnp.bfloat16), grad_up, grad_down)
```

```python
import functools

import jax
import jax.numpy as jnp
from jax import lax
from jax.experimental import pallas as pl
from jax.experimental.pallas import tpu as pltpu
from jax.sharding import PartitionSpec as P

MESH = pl.DeviceIdType.MESH
F32 = jnp.float32
BF16 = jnp.bfloat16
FIRST = (((0,), (0,)), ((), ()))
LAST = (((1,), (1,)), ((), ()))
PLAIN = (((1,), (0,)), ((), ()))


def dot(a, b, how=PLAIN):
    return lax.dot_general(a, b, how, preferred_element_type=F32)


def kernel(
    n_dp, n_ctx, n_tp, cap,
    ids_ref, codes_ref, tok_hbm, cot_hbm, up_hbm, down_hbm,
    mixed_hbm, gtok_hbm, gup_hbm, gdown_hbm,
    tok, cot, up, down, x_send, g_send, x_recv, g_recv, x_all, g_all,
    h_send, a_send, h_recv, a_recv, act, ghid,
    p_send, q_send, p_recv, q_recv, mixed, gtok, gup, gdown,
    in_sem, out_sem, xs, xr, gs, gr, hs, hr, as_, ar, cs, cr, ds, dr, ps, pr, qs, qr,
):
    d, c, t = lax.axis_index("dp"), lax.axis_index("ctx"), lax.axis_index("tp")
    n_blocks = n_dp * n_ctx
    me = d * n_ctx + c
    slots = n_ctx * cap

    loads = [
        pltpu.make_async_copy(src, dst, in_sem.at[i])
        for i, (src, dst) in enumerate(
            ((tok_hbm, tok), (cot_hbm, cot), (up_hbm.at[0], up), (down_hbm.at[0], down))
        )
    ]
    for load in loads:
        load.start()

    def block_dev(k):
        b = lax.rem(me + k, n_blocks)
        return b, {"dp": b // n_ctx, "ctx": lax.rem(b, n_ctx)}

    def tp_dev(k):
        j = lax.rem(t + k, n_tp)
        return j, {"tp": j}

    barrier = pltpu.get_barrier_semaphore()
    for k in range(1, n_blocks):
        pl.semaphore_signal(barrier, inc=1, device_id=block_dev(k)[1], device_id_type=MESH)
    for k in range(1, n_tp):
        pl.semaphore_signal(barrier, inc=1, device_id=tp_dev(k)[1], device_id_type=MESH)

    picks, rows = ids_ref.shape
    lane = lax.broadcasted_iota(jnp.int32, (slots, rows), 0)
    lane_e = jnp.zeros((slots, rows), jnp.int32)
    for e in range(1, n_ctx):
        lane_e = lane_e + (lane >= e * cap).astype(jnp.int32)
    lane_s = lane - lane_e * cap
    named = jnp.zeros((slots, rows), jnp.int32)
    code = jnp.zeros((slots, rows), jnp.int32)
    ids, codes = ids_ref[...], codes_ref[...]
    for k in range(picks):
        hit = ids[k : k + 1] == lane_e
        named = jnp.where(hit, 1, named)
        code = jnp.where(hit, codes[k : k + 1], code)
    earlier = (
        lax.broadcasted_iota(jnp.int32, (rows, rows), 0)
        < lax.broadcasted_iota(jnp.int32, (rows, rows), 1)
    )
    rank = dot(named.astype(F32).astype(BF16), earlier.astype(F32).astype(BF16))
    chosen = jnp.where(rank == lane_s.astype(F32), named, 0)
    code = chosen * code
    pick = chosen.astype(F32).astype(BF16)
    high = lax.shift_right_logical(code, 8)
    gate_hi = (high.astype(F32) * (1.0 / 128.0)).astype(BF16)
    gate_lo = ((code - high * 256).astype(F32) * (1.0 / 32768.0)).astype(BF16)

    pl.semaphore_wait(barrier, n_blocks - 1 + n_tp - 1)

    def spread(send, recv, send_sem, recv_sem):
        for k in range(1, n_blocks):
            b, dev = block_dev(k)
            pltpu.make_async_remote_copy(
                send.at[lax.rem(b, n_ctx)], recv.at[me], send_sem.at[k], recv_sem.at[me],
                device_id=dev, device_id_type=MESH,
            ).start()
        recv[me] = send[c]

    def arrived(recv, send_sem, recv_sem):
        for k in range(1, n_blocks):
            b, dev = block_dev(k)
            pltpu.make_async_remote_copy(
                recv.at[b], recv.at[b], send_sem.at[k], recv_sem.at[b],
                device_id=dev, device_id_type=MESH,
            ).wait_recv()

    def sent(send, send_sem):
        for k in range(1, n_blocks):
            b, dev = block_dev(k)
            pltpu.make_async_remote_copy(
                send.at[0], send.at[0], send_sem.at[k], send_sem.at[k],
                device_id=dev, device_id_type=MESH,
            ).wait_send()

    def put_blocks(ref, value, count):
        for b in range(count):
            ref[b] = value[b * cap : (b + 1) * cap].astype(BF16)

    def take_blocks(ref, count):
        return jnp.concatenate([ref[b].astype(F32) for b in range(count)], axis=0).astype(BF16)

    def tp_scatter(send, recv, send_sem, recv_sem):
        for k in range(1, n_tp):
            j, dev = tp_dev(k)
            pltpu.make_async_remote_copy(
                send.at[j], recv.at[t], send_sem.at[k], recv_sem.at[t],
                device_id=dev, device_id_type=MESH,
            ).start()

    def tp_gather(buf, send_sem, recv_sem):
        for k in range(1, n_tp):
            j, dev = tp_dev(k)
            pltpu.make_async_remote_copy(
                buf.at[t], buf.at[t], send_sem.at[k], recv_sem.at[t],
                device_id=dev, device_id_type=MESH,
            ).start()

    def tp_arrived(buf, send_sem, recv_sem):
        for k in range(1, n_tp):
            j, dev = tp_dev(k)
            pltpu.make_async_remote_copy(
                buf.at[j], buf.at[j], send_sem.at[k], recv_sem.at[j],
                device_id=dev, device_id_type=MESH,
            ).wait_recv()

    def tp_sent(buf, send_sem):
        for k in range(1, n_tp):
            j, dev = tp_dev(k)
            pltpu.make_async_remote_copy(
                buf.at[0], buf.at[0], send_sem.at[k], send_sem.at[k],
                device_id=dev, device_id_type=MESH,
            ).wait_send()

    loads[0].wait()
    put_blocks(x_send, dot(pick, tok[...]), n_ctx)
    spread(x_send, x_recv, xs, xr)
    loads[1].wait()
    put_blocks(g_send, dot(gate_hi, cot[...]) + dot(gate_lo, cot[...]), n_ctx)
    spread(g_send, g_recv, gs, gr)

    loads[2].wait()
    arrived(x_recv, xs, xr)
    x_all[...] = take_blocks(x_recv, n_blocks)
    piece = n_blocks * cap // n_tp
    part = dot(x_all[...], up[...])
    for j in range(n_tp):
        h_send[j] = part[j * piece : (j + 1) * piece].astype(BF16)
    tp_scatter(h_send, h_recv, hs, hr)
    loads[3].wait()
    arrived(g_recv, gs, gr)
    g_all[...] = take_blocks(g_recv, n_blocks)
    part = dot(g_all[...], down[...], LAST)
    for j in range(n_tp):
        a_send[j] = part[j * piece : (j + 1) * piece].astype(BF16)
    tp_scatter(a_send, a_recv, as_, ar)

    tp_arrived(h_recv, hs, hr)
    hidden = h_send[t].astype(F32)
    for k in range(1, n_tp):
        hidden = hidden + h_recv[lax.rem(t + k, n_tp)].astype(F32)
    sigma = 1.0 / (1.0 + jnp.exp(-hidden))
    act[t] = (hidden * sigma).astype(BF16)
    tp_gather(act, cs, cr)
    slope = sigma * (1.0 + hidden * (1.0 - sigma))
    tp_arrived(a_recv, as_, ar)
    grad_act = a_send[t].astype(F32)
    for k in range(1, n_tp):
        grad_act = grad_act + a_recv[lax.rem(t + k, n_tp)].astype(F32)
    ghid[t] = (grad_act * slope).astype(BF16)
    tp_gather(ghid, ds, dr)

    def spread_back(send, recv, send_sem, recv_sem):
        for k in range(1, n_blocks):
            b, dev = block_dev(k)
            pltpu.make_async_remote_copy(
                send.at[b], recv.at[me], send_sem.at[k], recv_sem.at[me],
                device_id=dev, device_id_type=MESH,
            ).start()
        recv[me] = send[me]

    def whole(buf):
        return jnp.concatenate([buf[j] for j in range(n_tp)], axis=0)

    tp_arrived(act, cs, cr)
    act_all = whole(act)
    put_blocks(p_send, dot(act_all, down[...]), n_blocks)
    spread_back(p_send, p_recv, ps, pr)
    tp_arrived(ghid, ds, dr)
    ghid_all = whole(ghid)
    put_blocks(q_send, dot(ghid_all, up[...], LAST), n_blocks)
    spread_back(q_send, q_recv, qs, qr)

    gdown[...] = dot(act_all, g_all[...], FIRST).astype(BF16)
    stores = [pltpu.make_async_copy(gdown, gdown_hbm.at[0], out_sem.at[0])]
    stores[-1].start()
    gup[...] = dot(x_all[...], ghid_all, FIRST).astype(BF16)
    stores.append(pltpu.make_async_copy(gup, gup_hbm.at[0], out_sem.at[1]))
    stores[-1].start()

    arrived(p_recv, ps, pr)
    got = take_blocks(p_recv, n_blocks)
    mixed[...] = (
        dot(jnp.concatenate([gate_hi] * n_dp, axis=0), got, FIRST)
        + dot(jnp.concatenate([gate_lo] * n_dp, axis=0), got, FIRST)
    ).astype(BF16)
    stores.append(pltpu.make_async_copy(mixed, mixed_hbm, out_sem.at[2]))
    stores[-1].start()
    arrived(q_recv, qs, qr)
    got = take_blocks(q_recv, n_blocks)
    gtok[...] = dot(jnp.concatenate([pick] * n_dp, axis=0), got, FIRST).astype(BF16)
    stores.append(pltpu.make_async_copy(gtok, gtok_hbm, out_sem.at[3]))
    stores[-1].start()

    sent(x_send, xs)
    sent(g_send, gs)
    tp_sent(h_recv, hs)
    tp_sent(a_recv, as_)
    tp_sent(act, cs)
    tp_sent(ghid, ds)
    sent(p_send, ps)
    sent(q_send, qs)
    for store in stores:
        store.wait()


def body(n_dp, n_ctx, n_tp, tokens, expert_ids, gate_codes, up_weight, down_weight, cotangent):
    rows, feats = tokens.shape
    hid = up_weight.shape[2]
    cap = rows // 16
    blocks = n_dp * n_ctx
    total = blocks * cap
    piece = total // n_tp
    any_ = pl.BlockSpec(memory_space=pl.ANY)
    vmem = pl.BlockSpec(memory_space=pltpu.VMEM)
    dma = pltpu.SemaphoreType.DMA

    def buf(*shape):
        return pltpu.VMEM(shape, BF16)

    return pl.pallas_call(
        functools.partial(kernel, n_dp, n_ctx, n_tp, cap),
        out_shape=[
            jax.ShapeDtypeStruct(a.shape, BF16)
            for a in (tokens, tokens, up_weight, down_weight)
        ],
        in_specs=[vmem, vmem, any_, any_, any_, any_],
        out_specs=[any_] * 4,
        scratch_shapes=[
            buf(rows, feats), buf(rows, feats), buf(feats, hid), buf(hid, feats),
            buf(n_ctx, cap, feats), buf(n_ctx, cap, feats),
            buf(blocks, cap, feats), buf(blocks, cap, feats),
            buf(total, feats), buf(total, feats),
            buf(n_tp, piece, hid), buf(n_tp, piece, hid),
            buf(n_tp, piece, hid), buf(n_tp, piece, hid),
            buf(n_tp, piece, hid), buf(n_tp, piece, hid),
            buf(blocks, cap, feats), buf(blocks, cap, feats),
            buf(blocks, cap, feats), buf(blocks, cap, feats),
            buf(rows, feats), buf(rows, feats), buf(feats, hid), buf(hid, feats),
            dma((4,)), dma((4,)),
            dma((blocks,)), dma((blocks,)), dma((blocks,)), dma((blocks,)),
            dma((n_tp,)), dma((n_tp,)), dma((n_tp,)), dma((n_tp,)),
            dma((n_tp,)), dma((n_tp,)), dma((n_tp,)), dma((n_tp,)),
            dma((blocks,)), dma((blocks,)), dma((blocks,)), dma((blocks,)),
        ],
        compiler_params=pltpu.CompilerParams(collective_id=0, has_side_effects=True),
        name="expert_layer",
    )(expert_ids.T, gate_codes.T, tokens, cotangent, up_weight, down_weight)


def solution(mesh):
    sizes = [mesh.shape[name] for name in ("dp", "ctx", "tp")]
    return jax.shard_map(
        functools.partial(body, *sizes),
        mesh=mesh,
        in_specs=(
            P(("dp", "ctx"), "tp"),
            P(("dp", "ctx"), None),
            P(("dp", "ctx"), None),
            P("ctx", "tp", "dp"),
            P("ctx", "dp", "tp"),
            P(("dp", "ctx"), "tp"),
        ),
        out_specs=(
            P(("dp", "ctx"), "tp"),
            P(("dp", "ctx"), "tp"),
            P("ctx", "tp", "dp"),
            P("ctx", "dp", "tp"),
        ),
        check_vma=False,
    )
```

```python
import functools

import jax
import jax.numpy as jnp
from jax import lax
from jax.experimental import pallas as pl
from jax.experimental.pallas import tpu as pltpu
from jax.sharding import PartitionSpec as P

MESH = pl.DeviceIdType.MESH
F32 = jnp.float32
BF16 = jnp.bfloat16
FIRST = (((0,), (0,)), ((), ()))
LAST = (((1,), (1,)), ((), ()))
PLAIN = (((1,), (0,)), ((), ()))


def dot(a, b, how=PLAIN):
    return lax.dot_general(a, b, how, preferred_element_type=F32)


def kernel(
    n_dp, n_ctx, n_tp, cap,
    ids_ref, codes_ref, tok_hbm, cot_hbm, up_hbm, down_hbm,
    mixed, gtok, gup, gdown,
    tok, cot, up, down, x_send, g_send, x_recv, g_recv, x_all, g_all,
    h_send, a_send, h_recv, a_recv, act, ghid, act_all, ghid_all,
    p_send, q_send, p_recv, q_recv,
    in_sem, xs, xr, gs, gr, hs, hr, as_, ar, cs, cr, ds, dr, ps, pr, qs, qr,
):
    d, c, t = lax.axis_index("dp"), lax.axis_index("ctx"), lax.axis_index("tp")
    n_blocks = n_dp * n_ctx
    me = d * n_ctx + c
    slots = n_ctx * cap

    loads = [
        pltpu.make_async_copy(src, dst, in_sem.at[i])
        for i, (src, dst) in enumerate(
            ((tok_hbm, tok), (cot_hbm, cot), (up_hbm.at[0], up), (down_hbm.at[0], down))
        )
    ]
    for load in loads:
        load.start()

    def block_dev(k):
        b = lax.rem(me + k, n_blocks)
        return b, {"dp": b // n_ctx, "ctx": lax.rem(b, n_ctx)}

    def tp_dev(k):
        j = lax.rem(t + k, n_tp)
        return j, {"tp": j}

    barrier = pltpu.get_barrier_semaphore()
    for k in range(1, n_blocks):
        pl.semaphore_signal(barrier, inc=1, device_id=block_dev(k)[1], device_id_type=MESH)
    for k in range(1, n_tp):
        pl.semaphore_signal(barrier, inc=1, device_id=tp_dev(k)[1], device_id_type=MESH)

    picks, rows = ids_ref.shape
    lane = lax.broadcasted_iota(jnp.int32, (slots, rows), 0)
    lane_e = jnp.zeros((slots, rows), jnp.int32)
    for e in range(1, n_ctx):
        lane_e = lane_e + (lane >= e * cap).astype(jnp.int32)
    lane_s = lane - lane_e * cap
    named = jnp.zeros((slots, rows), jnp.int32)
    code = jnp.zeros((slots, rows), jnp.int32)
    ids, codes = ids_ref[...], codes_ref[...]
    for k in range(picks):
        hit = ids[k : k + 1] == lane_e
        named = jnp.where(hit, 1, named)
        code = jnp.where(hit, codes[k : k + 1], code)
    earlier = (
        lax.broadcasted_iota(jnp.int32, (rows, rows), 0)
        < lax.broadcasted_iota(jnp.int32, (rows, rows), 1)
    )
    rank = dot(named.astype(F32).astype(BF16), earlier.astype(F32).astype(BF16))
    chosen = jnp.where(rank == lane_s.astype(F32), named, 0)
    code = chosen * code
    pick = chosen.astype(F32).astype(BF16)
    high = lax.shift_right_logical(code, 8)
    gate_hi = (high.astype(F32) * (1.0 / 128.0)).astype(BF16)
    gate_lo = ((code - high * 256).astype(F32) * (1.0 / 32768.0)).astype(BF16)

    pl.semaphore_wait(barrier, n_blocks - 1 + n_tp - 1)

    def groups_dev(g, cc):
        return {"dp": g, "ctx": cc}

    def others(k):
        return range(1 if k == 0 else 0, n_ctx)

    def to(k, m):
        return lax.rem(d + k, n_dp), lax.rem(c + m, n_ctx)

    def spread(send, recv, send_sem, recv_sem, k, back=False):
        for m in others(k):
            g, e = to(k, m)
            src = send.at[g * n_ctx + e] if back else send.at[e]
            pltpu.make_async_remote_copy(
                src, recv.at[me], send_sem.at[k * n_ctx + m], recv_sem.at[me],
                device_id=groups_dev(g, e), device_id_type=MESH,
            ).start()
        if k == 0:
            recv[me] = send[me] if back else send[c]

    def arrived(recv, recv_sem, k):
        g = lax.rem(d + n_dp - k, n_dp)
        for m in others(k):
            e = lax.rem(c + m, n_ctx)
            b = g * n_ctx + e
            pltpu.make_async_remote_copy(
                recv.at[b], recv.at[b], recv_sem.at[b], recv_sem.at[b],
                device_id=groups_dev(g, e), device_id_type=MESH,
            ).wait_recv()
        return g

    def sent(send, send_sem):
        for k in range(n_dp):
            for m in others(k):
                g, e = to(k, m)
                i = k * n_ctx + m
                pltpu.make_async_remote_copy(
                    send.at[0], send.at[0], send_sem.at[i], send_sem.at[i],
                    device_id=groups_dev(g, e), device_id_type=MESH,
                ).wait_send()

    def put_blocks(ref, first, value, count):
        for b in range(count):
            ref[first + b] = value[b * cap : (b + 1) * cap].astype(BF16)

    def take_blocks(ref, first, count):
        return jnp.concatenate(
            [ref[first + b].astype(F32) for b in range(count)], axis=0
        ).astype(BF16)

    def tp_scatter(send, recv, send_sem, recv_sem, k):
        for m in range(1, n_tp):
            j, dev = tp_dev(m)
            pltpu.make_async_remote_copy(
                send.at[k, j], recv.at[k, t], send_sem.at[k, m], recv_sem.at[k, t],
                device_id=dev, device_id_type=MESH,
            ).start()

    def tp_gather(buf, send_sem, recv_sem, k):
        for m in range(1, n_tp):
            j, dev = tp_dev(m)
            pltpu.make_async_remote_copy(
                buf.at[k, t], buf.at[k, t], send_sem.at[k, m], recv_sem.at[k, t],
                device_id=dev, device_id_type=MESH,
            ).start()

    def tp_arrived(buf, recv_sem, k):
        for m in range(1, n_tp):
            j, dev = tp_dev(m)
            pltpu.make_async_remote_copy(
                buf.at[k, j], buf.at[k, j], recv_sem.at[k, j], recv_sem.at[k, j],
                device_id=dev, device_id_type=MESH,
            ).wait_recv()

    def tp_sent(buf, send_sem):
        for k in range(n_dp):
            for m in range(1, n_tp):
                j, dev = tp_dev(m)
                pltpu.make_async_remote_copy(
                    buf.at[k, 0], buf.at[k, 0], send_sem.at[k, m], send_sem.at[k, m],
                    device_id=dev, device_id_type=MESH,
                ).wait_send()

    forth, back = list(range(n_dp)), list(reversed(range(n_dp)))
    loads[0].wait()
    put_blocks(x_send, 0, dot(pick, tok[...]), n_ctx)
    for k in forth:
        spread(x_send, x_recv, xs, xr, k)
    loads[1].wait()
    put_blocks(g_send, 0, dot(gate_hi, cot[...]) + dot(gate_lo, cot[...]), n_ctx)
    for k in back:
        spread(g_send, g_recv, gs, gr, k)

    group = slots
    piece = group // n_tp

    def put_pieces(ref, k, value):
        for j in range(n_tp):
            ref[k, j] = value[j * piece : (j + 1) * piece].astype(BF16)

    def total(send, recv, k):
        value = send[k, t].astype(F32)
        for m in range(1, n_tp):
            value = value + recv[k, lax.rem(t + m, n_tp)].astype(F32)
        return value

    loads[2].wait()
    for k in forth:
        g = arrived(x_recv, xr, k)
        x_all[k * group : (k + 1) * group] = take_blocks(x_recv, g * n_ctx, n_ctx)
        put_pieces(h_send, k, dot(x_all[k * group : (k + 1) * group], up[...]))
        tp_scatter(h_send, h_recv, hs, hr, k)
    loads[3].wait()
    for k in back:
        g = arrived(g_recv, gr, k)
        g_all[k * group : (k + 1) * group] = take_blocks(g_recv, g * n_ctx, n_ctx)
        put_pieces(a_send, k, dot(g_all[k * group : (k + 1) * group], down[...], LAST))
        tp_scatter(a_send, a_recv, as_, ar, k)

    for k in back:
        tp_arrived(h_recv, hr, k)
        hidden = total(h_send, h_recv, k)
        sigma = 1.0 / (1.0 + jnp.exp(-hidden))
        act[k, t] = (hidden * sigma).astype(BF16)
        tp_gather(act, cs, cr, k)
        slope = sigma * (1.0 + hidden * (1.0 - sigma))
        tp_arrived(a_recv, ar, k)
        ghid[k, t] = (total(a_send, a_recv, k) * slope).astype(BF16)
        tp_gather(ghid, ds, dr, k)

    def whole(buf, k):
        return jnp.concatenate([buf[k, j].astype(F32) for j in range(n_tp)], axis=0).astype(BF16)

    for k in back:
        rows_k = slice(k * group, (k + 1) * group)
        first = lax.rem(d + n_dp - k, n_dp) * n_ctx
        to_k = (n_dp - k) % n_dp
        tp_arrived(act, cr, k)
        act_all[rows_k] = whole(act, k)
        put_blocks(p_send, first, dot(act_all[rows_k], down[...]), n_ctx)
        spread(p_send, p_recv, ps, pr, to_k, back=True)
        tp_arrived(ghid, dr, k)
        ghid_all[rows_k] = whole(ghid, k)
        put_blocks(q_send, first, dot(ghid_all[rows_k], up[...], LAST), n_ctx)
        spread(q_send, q_recv, qs, qr, to_k, back=True)

    gdown[0] = dot(act_all[...], g_all[...], FIRST).astype(BF16)
    gup[0] = dot(x_all[...], ghid_all[...], FIRST).astype(BF16)

    for k in back:
        arrived(p_recv, pr, k)
    out = jnp.zeros(mixed.shape, F32)
    for g in range(n_dp):
        got = take_blocks(p_recv, g * n_ctx, n_ctx)
        out = out + dot(gate_hi, got, FIRST) + dot(gate_lo, got, FIRST)
    mixed[...] = out.astype(BF16)
    for k in back:
        arrived(q_recv, qr, k)
    out = jnp.zeros(gtok.shape, F32)
    for g in range(n_dp):
        out = out + dot(pick, take_blocks(q_recv, g * n_ctx, n_ctx), FIRST)
    gtok[...] = out.astype(BF16)

    sent(x_send, xs)
    sent(g_send, gs)
    tp_sent(h_recv, hs)
    tp_sent(a_recv, as_)
    tp_sent(act, cs)
    tp_sent(ghid, ds)
    sent(p_send, ps)
    sent(q_send, qs)


def store(*refs):
    sem = refs[-1]
    copies = [
        pltpu.make_async_copy(src, dst, sem.at[i])
        for i, (src, dst) in enumerate(zip(refs[:4], refs[4:8]))
    ]
    for copy in copies:
        copy.start()
    for copy in copies:
        copy.wait()


def body(n_dp, n_ctx, n_tp, tokens, expert_ids, gate_codes, up_weight, down_weight, cotangent):
    rows, feats = tokens.shape
    hid = up_weight.shape[2]
    cap = rows // 16
    blocks = n_dp * n_ctx
    total = blocks * cap
    piece = n_ctx * cap // n_tp
    any_ = pl.BlockSpec(memory_space=pl.ANY)
    vmem = pl.BlockSpec(memory_space=pltpu.VMEM)
    dma = pltpu.SemaphoreType.DMA

    def buf(*shape):
        return pltpu.VMEM(shape, BF16)

    tp_sems = [dma((n_dp, n_tp))] * 8
    results = pl.pallas_call(
        functools.partial(kernel, n_dp, n_ctx, n_tp, cap),
        out_shape=[
            buf(*a.shape) for a in (tokens, tokens, up_weight, down_weight)
        ],
        in_specs=[vmem, vmem, any_, any_, any_, any_],
        out_specs=[vmem] * 4,
        scratch_shapes=[
            buf(rows, feats), buf(rows, feats), buf(feats, hid), buf(hid, feats),
            buf(n_ctx, cap, feats), buf(n_ctx, cap, feats),
            buf(blocks, cap, feats), buf(blocks, cap, feats),
            buf(total, feats), buf(total, feats),
            buf(n_dp, n_tp, piece, hid), buf(n_dp, n_tp, piece, hid),
            buf(n_dp, n_tp, piece, hid), buf(n_dp, n_tp, piece, hid),
            buf(n_dp, n_tp, piece, hid), buf(n_dp, n_tp, piece, hid),
            buf(total, hid), buf(total, hid),
            buf(blocks, cap, feats), buf(blocks, cap, feats),
            buf(blocks, cap, feats), buf(blocks, cap, feats),
            dma((4,)),
            dma((blocks,)), dma((blocks,)), dma((blocks,)), dma((blocks,)),
            *tp_sems,
            dma((blocks,)), dma((blocks,)), dma((blocks,)), dma((blocks,)),
        ],
        compiler_params=pltpu.CompilerParams(
            collective_id=0, has_side_effects=True, vmem_limit_bytes=58 * 2**20
        ),
        name="expert_layer",
    )(expert_ids.T, gate_codes.T, tokens, cotangent, up_weight, down_weight)
    return tuple(
        pl.pallas_call(
            store,
            out_shape=[
                jax.ShapeDtypeStruct(a.shape, BF16)
                for a in (tokens, tokens, up_weight, down_weight)
            ],
            in_specs=[vmem] * 4,
            out_specs=[any_] * 4,
            scratch_shapes=[dma((4,))],
            compiler_params=pltpu.CompilerParams(vmem_limit_bytes=2**20),
            name="store",
        )(*[pltpu.with_memory_space_constraint(a, pltpu.VMEM) for a in results])
    )


def solution(mesh):
    sizes = [mesh.shape[name] for name in ("dp", "ctx", "tp")]
    return jax.shard_map(
        functools.partial(body, *sizes),
        mesh=mesh,
        in_specs=(
            P(("dp", "ctx"), "tp"),
            P(("dp", "ctx"), None),
            P(("dp", "ctx"), None),
            P("ctx", "tp", "dp"),
            P("ctx", "dp", "tp"),
            P(("dp", "ctx"), "tp"),
        ),
        out_specs=(
            P(("dp", "ctx"), "tp"),
            P(("dp", "ctx"), "tp"),
            P("ctx", "tp", "dp"),
            P("ctx", "dp", "tp"),
        ),
        check_vma=False,
    )
```

```python
import functools

import jax
import jax.numpy as jnp
from jax import lax
from jax.experimental import pallas as pl
from jax.experimental.pallas import tpu as pltpu
from jax.sharding import PartitionSpec as P

MESH = pl.DeviceIdType.MESH
F32 = jnp.float32
BF16 = jnp.bfloat16
FIRST = (((0,), (0,)), ((), ()))
LAST = (((1,), (1,)), ((), ()))
PLAIN = (((1,), (0,)), ((), ()))


def dot(a, b, how=PLAIN):
    return lax.dot_general(a, b, how, preferred_element_type=F32)


def kernel(
    n_dp, n_ctx, n_tp, cap,
    ids_ref, codes_ref, tok_hbm, cot_hbm, up_hbm, down_hbm,
    mixed, gtok, gup, gdown,
    tok, cot, up, down, x_send, g_send, x_recv, g_recv, x_all, g_all,
    h_send, a_send, h_recv, a_recv, act, ghid, act_all, ghid_all,
    p_send, q_send, p_recv, q_recv,
    in_sem, xs, xr, gs, gr, hs, hr, as_, ar, cs, cr, ds, dr, ps, pr, qs, qr,
):
    d, c, t = lax.axis_index("dp"), lax.axis_index("ctx"), lax.axis_index("tp")
    n_blocks = n_dp * n_ctx
    me = d * n_ctx + c
    slots = n_ctx * cap

    loads = [
        pltpu.make_async_copy(src, dst, in_sem.at[i])
        for i, (src, dst) in enumerate(
            ((tok_hbm, tok), (cot_hbm, cot), (up_hbm.at[0], up), (down_hbm.at[0], down))
        )
    ]
    for load in loads:
        load.start()

    def block_dev(k):
        b = lax.rem(me + k, n_blocks)
        return b, {"dp": b // n_ctx, "ctx": lax.rem(b, n_ctx)}

    def tp_dev(k):
        j = lax.rem(t + k, n_tp)
        return j, {"tp": j}

    barrier = pltpu.get_barrier_semaphore()
    for k in range(1, n_blocks):
        pl.semaphore_signal(barrier, inc=1, device_id=block_dev(k)[1], device_id_type=MESH)
    for k in range(1, n_tp):
        pl.semaphore_signal(barrier, inc=1, device_id=tp_dev(k)[1], device_id_type=MESH)

    picks, rows = ids_ref.shape
    lane = lax.broadcasted_iota(jnp.int32, (slots, rows), 0)
    lane_e = jnp.zeros((slots, rows), jnp.int32)
    for e in range(1, n_ctx):
        lane_e = lane_e + (lane >= e * cap).astype(jnp.int32)
    lane_s = lane - lane_e * cap
    named = jnp.zeros((slots, rows), jnp.int32)
    code = jnp.zeros((slots, rows), jnp.int32)
    ids, codes = ids_ref[...], codes_ref[...]
    for k in range(picks):
        hit = ids[k : k + 1] == lane_e
        named = jnp.where(hit, 1, named)
        code = jnp.where(hit, codes[k : k + 1], code)
    earlier = (
        lax.broadcasted_iota(jnp.int32, (rows, rows), 0)
        < lax.broadcasted_iota(jnp.int32, (rows, rows), 1)
    )
    rank = dot(named.astype(F32).astype(BF16), earlier.astype(F32).astype(BF16))
    chosen = jnp.where(rank == lane_s.astype(F32), named, 0)
    code = chosen * code
    pick = chosen.astype(F32).astype(BF16)
    high = lax.shift_right_logical(code, 8)
    gate_hi = (high.astype(F32) * (1.0 / 128.0)).astype(BF16)
    gate_lo = ((code - high * 256).astype(F32) * (1.0 / 32768.0)).astype(BF16)

    def groups_dev(g, cc):
        return {"dp": g, "ctx": cc}

    def others(k):
        return range(1 if k == 0 else 0, n_ctx)

    def to(k, m):
        return lax.rem(d + k, n_dp), lax.rem(c + m, n_ctx)

    def spread(send, recv, send_sem, recv_sem, k, back=False):
        for m in others(k):
            g, e = to(k, m)
            src = send.at[g * n_ctx + e] if back else send.at[e]
            pltpu.make_async_remote_copy(
                src, recv.at[me], send_sem.at[k * n_ctx + m], recv_sem.at[me],
                device_id=groups_dev(g, e), device_id_type=MESH,
            ).start()
        if k == 0:
            recv[me] = send[me] if back else send[c]

    def arrived(recv, recv_sem, k):
        g = lax.rem(d + n_dp - k, n_dp)
        for m in others(k):
            e = lax.rem(c + m, n_ctx)
            b = g * n_ctx + e
            pltpu.make_async_remote_copy(
                recv.at[b], recv.at[b], recv_sem.at[b], recv_sem.at[b],
                device_id=groups_dev(g, e), device_id_type=MESH,
            ).wait_recv()
        return g

    def sent(send, send_sem):
        for k in range(n_dp):
            for m in others(k):
                g, e = to(k, m)
                i = k * n_ctx + m
                pltpu.make_async_remote_copy(
                    send.at[0], send.at[0], send_sem.at[i], send_sem.at[i],
                    device_id=groups_dev(g, e), device_id_type=MESH,
                ).wait_send()

    def put_blocks(ref, first, value, count):
        for b in range(count):
            ref[first + b] = value[b * cap : (b + 1) * cap].astype(BF16)

    def take_blocks(ref, first, count):
        return jnp.concatenate(
            [ref[first + b].astype(F32) for b in range(count)], axis=0
        ).astype(BF16)

    def tp_scatter(send, recv, send_sem, recv_sem, k):
        for m in range(1, n_tp):
            j, dev = tp_dev(m)
            pltpu.make_async_remote_copy(
                send.at[k, j], recv.at[k, t], send_sem.at[k, m], recv_sem.at[k, t],
                device_id=dev, device_id_type=MESH,
            ).start()

    def tp_gather(buf, send_sem, recv_sem, k):
        for m in range(1, n_tp):
            j, dev = tp_dev(m)
            pltpu.make_async_remote_copy(
                buf.at[k, t], buf.at[k, t], send_sem.at[k, m], recv_sem.at[k, t],
                device_id=dev, device_id_type=MESH,
            ).start()

    def tp_arrived(buf, recv_sem, k):
        for m in range(1, n_tp):
            j, dev = tp_dev(m)
            pltpu.make_async_remote_copy(
                buf.at[k, j], buf.at[k, j], recv_sem.at[k, j], recv_sem.at[k, j],
                device_id=dev, device_id_type=MESH,
            ).wait_recv()

    def tp_sent(buf, send_sem):
        for k in range(n_dp):
            for m in range(1, n_tp):
                j, dev = tp_dev(m)
                pltpu.make_async_remote_copy(
                    buf.at[k, 0], buf.at[k, 0], send_sem.at[k, m], send_sem.at[k, m],
                    device_id=dev, device_id_type=MESH,
                ).wait_send()

    forth, back = list(range(n_dp)), list(reversed(range(n_dp)))
    loads[0].wait()
    put_blocks(x_send, 0, dot(pick, tok[...]), n_ctx)
    pl.semaphore_wait(barrier, n_blocks - 1 + n_tp - 1)
    for k in forth:
        spread(x_send, x_recv, xs, xr, k)
    loads[1].wait()
    put_blocks(g_send, 0, dot(gate_hi, cot[...]) + dot(gate_lo, cot[...]), n_ctx)
    for k in back:
        spread(g_send, g_recv, gs, gr, k)

    group = slots
    piece = group // n_tp

    def put_pieces(ref, k, value):
        for j in range(n_tp):
            ref[k, j] = value[j * piece : (j + 1) * piece].astype(BF16)

    def total(send, recv, k):
        value = send[k, t].astype(F32)
        for m in range(1, n_tp):
            value = value + recv[k, lax.rem(t + m, n_tp)].astype(F32)
        return value

    loads[2].wait()
    for k in forth:
        g = arrived(x_recv, xr, k)
        x_all[k * group : (k + 1) * group] = take_blocks(x_recv, g * n_ctx, n_ctx)
        put_pieces(h_send, k, dot(x_all[k * group : (k + 1) * group], up[...]))
        tp_scatter(h_send, h_recv, hs, hr, k)
    slopes = [None] * n_dp
    for k in forth:
        tp_arrived(h_recv, hr, k)
        hidden = total(h_send, h_recv, k)
        sigma = 1.0 / (1.0 + jnp.exp(-hidden))
        act[k, t] = (hidden * sigma).astype(BF16)
        tp_gather(act, cs, cr, k)
        slopes[k] = sigma * (1.0 + hidden * (1.0 - sigma))
    loads[3].wait()
    for k in back:
        g = arrived(g_recv, gr, k)
        g_all[k * group : (k + 1) * group] = take_blocks(g_recv, g * n_ctx, n_ctx)
        put_pieces(a_send, k, dot(g_all[k * group : (k + 1) * group], down[...], LAST))
        tp_scatter(a_send, a_recv, as_, ar, k)

    def whole(buf, k):
        return jnp.concatenate([buf[k, j].astype(F32) for j in range(n_tp)], axis=0).astype(BF16)

    def home(k):
        return lax.rem(d + n_dp - k, n_dp) * n_ctx, (n_dp - k) % n_dp

    for k in back:
        rows_k = slice(k * group, (k + 1) * group)
        first, to_k = home(k)
        tp_arrived(act, cr, k)
        act_all[rows_k] = whole(act, k)
        put_blocks(p_send, first, dot(act_all[rows_k], down[...]), n_ctx)
        spread(p_send, p_recv, ps, pr, to_k, back=True)
    for k in back:
        tp_arrived(a_recv, ar, k)
        ghid[k, t] = (total(a_send, a_recv, k) * slopes[k]).astype(BF16)
        tp_gather(ghid, ds, dr, k)
    for k in back:
        rows_k = slice(k * group, (k + 1) * group)
        first, to_k = home(k)
        tp_arrived(ghid, dr, k)
        ghid_all[rows_k] = whole(ghid, k)
        put_blocks(q_send, first, dot(ghid_all[rows_k], up[...], LAST), n_ctx)
        spread(q_send, q_recv, qs, qr, to_k, back=True)

    gdown[0] = dot(act_all[...], g_all[...], FIRST).astype(BF16)
    gup[0] = dot(x_all[...], ghid_all[...], FIRST).astype(BF16)

    for k in back:
        arrived(p_recv, pr, k)
    out = jnp.zeros(mixed.shape, F32)
    for g in range(n_dp):
        got = take_blocks(p_recv, g * n_ctx, n_ctx)
        out = out + dot(gate_hi, got, FIRST) + dot(gate_lo, got, FIRST)
    mixed[...] = out.astype(BF16)
    for k in back:
        arrived(q_recv, qr, k)
    out = jnp.zeros(gtok.shape, F32)
    for g in range(n_dp):
        out = out + dot(pick, take_blocks(q_recv, g * n_ctx, n_ctx), FIRST)
    gtok[...] = out.astype(BF16)

    sent(x_send, xs)
    sent(g_send, gs)
    tp_sent(h_recv, hs)
    tp_sent(a_recv, as_)
    tp_sent(act, cs)
    tp_sent(ghid, ds)
    sent(p_send, ps)
    sent(q_send, qs)


def store(*refs):
    sem = refs[-1]
    copies = [
        pltpu.make_async_copy(src, dst, sem.at[i])
        for i, (src, dst) in enumerate(zip(refs[:4], refs[4:8]))
    ]
    for copy in copies:
        copy.start()
    for copy in copies:
        copy.wait()


def body(n_dp, n_ctx, n_tp, tokens, expert_ids, gate_codes, up_weight, down_weight, cotangent):
    rows, feats = tokens.shape
    hid = up_weight.shape[2]
    cap = rows // 16
    blocks = n_dp * n_ctx
    total = blocks * cap
    piece = n_ctx * cap // n_tp
    any_ = pl.BlockSpec(memory_space=pl.ANY)
    vmem = pl.BlockSpec(memory_space=pltpu.VMEM)
    dma = pltpu.SemaphoreType.DMA

    def buf(*shape):
        return pltpu.VMEM(shape, BF16)

    tp_sems = [dma((n_dp, n_tp))] * 8
    results = pl.pallas_call(
        functools.partial(kernel, n_dp, n_ctx, n_tp, cap),
        out_shape=[
            buf(*a.shape) for a in (tokens, tokens, up_weight, down_weight)
        ],
        in_specs=[vmem, vmem, any_, any_, any_, any_],
        out_specs=[vmem] * 4,
        scratch_shapes=[
            buf(rows, feats), buf(rows, feats), buf(feats, hid), buf(hid, feats),
            buf(n_ctx, cap, feats), buf(n_ctx, cap, feats),
            buf(blocks, cap, feats), buf(blocks, cap, feats),
            buf(total, feats), buf(total, feats),
            buf(n_dp, n_tp, piece, hid), buf(n_dp, n_tp, piece, hid),
            buf(n_dp, n_tp, piece, hid), buf(n_dp, n_tp, piece, hid),
            buf(n_dp, n_tp, piece, hid), buf(n_dp, n_tp, piece, hid),
            buf(total, hid), buf(total, hid),
            buf(blocks, cap, feats), buf(blocks, cap, feats),
            buf(blocks, cap, feats), buf(blocks, cap, feats),
            dma((4,)),
            dma((blocks,)), dma((blocks,)), dma((blocks,)), dma((blocks,)),
            *tp_sems,
            dma((blocks,)), dma((blocks,)), dma((blocks,)), dma((blocks,)),
        ],
        compiler_params=pltpu.CompilerParams(
            collective_id=0, has_side_effects=True, vmem_limit_bytes=58 * 2**20
        ),
        name="expert_layer",
    )(expert_ids.T, gate_codes.T, tokens, cotangent, up_weight, down_weight)
    return tuple(
        pl.pallas_call(
            store,
            out_shape=[
                jax.ShapeDtypeStruct(a.shape, BF16)
                for a in (tokens, tokens, up_weight, down_weight)
            ],
            in_specs=[vmem] * 4,
            out_specs=[any_] * 4,
            scratch_shapes=[dma((4,))],
            compiler_params=pltpu.CompilerParams(vmem_limit_bytes=2**20),
            name="store",
        )(*[pltpu.with_memory_space_constraint(a, pltpu.VMEM) for a in results])
    )


def solution(mesh):
    sizes = [mesh.shape[name] for name in ("dp", "ctx", "tp")]
    return jax.shard_map(
        functools.partial(body, *sizes),
        mesh=mesh,
        in_specs=(
            P(("dp", "ctx"), "tp"),
            P(("dp", "ctx"), None),
            P(("dp", "ctx"), None),
            P("ctx", "tp", "dp"),
            P("ctx", "dp", "tp"),
            P(("dp", "ctx"), "tp"),
        ),
        out_specs=(
            P(("dp", "ctx"), "tp"),
            P(("dp", "ctx"), "tp"),
            P("ctx", "tp", "dp"),
            P("ctx", "dp", "tp"),
        ),
        check_vma=False,
    )
```
